32 devices in a mesh: seq: 16 (over z, y, core), head: 2 (over x).
Axes of the slice: x: 2, y: 2, z: 4, core: 2. Of those that a mesh axis runs over, the one named last changes fastest.
Arguments:
- qkv: bfloat16 [3, 2048, 1024], P(None, ('seq', 'head')), may hold values from -128 to 128
- token_rate: float32 [2048, 2], P('seq', 'head'), may hold values from 0.1 to 1
- head_rate: float32 [2], P('head'), may hold values from 0.5 to 2
- fast_state: float32 [3, 2, 512, 512], P(None, 'head', 'seq'), may hold values from -0.25 to 0.25
Outputs:
- combined: bfloat16 [2048, 1024], P(('seq', 'head'))
- new_state: float32 [3, 2, 512, 512], P(None, 'head', 'seq')
The draws below stay inside these ranges and needn't reach their ends.
All inputs are finite; a program needn't handle non-finite values.
Results may differ from the reference program's by a relative error of at most 0.017.
Values may be sent and summed in bfloat16 or wider, within the bound.
A program may use at most 64 MiB of HBM per device.

```python
import math
import jax
import jax.numpy as jnp
from jax import lax

HD = 512
FH = 512
HEADS = 2
TOK_DEV = 128
TOKENS = 2048
WINDOW = 1024
NS_STEPS = 2


def draw_qkv(key, part):
    feature_count = HEADS * HD
    branches = jax.random.split(key, 1)
    drawn = jnp.clip(jax.random.normal(branches[0], (3, TOKENS, feature_count), jnp.float32), -6.0, 6.0)
    drawn = drawn * jnp.array([1.0, 1.0, 2.0], jnp.float32)[:, None, None]
    return drawn.astype(jnp.bfloat16)


def steps_of(key, shape, cuts, smallest, high):
    level = 1.0
    for position, blocks in cuts:
        steps = jax.random.uniform(jax.random.fold_in(jax.random.fold_in(key, 6), position), (blocks,), jnp.float32, smallest / len(cuts), high / len(cuts))
        level = level * jnp.repeat(jnp.exp(steps), shape[position] // blocks).reshape((-1,) + (1,) * (len(shape) - 1 - position))
    return level


def bell_draw(rng, shape, width, limit, cuts=(), kind=jnp.bfloat16):
    loudness = steps_of(rng, shape, cuts, -0.22, 0.18) if cuts else 1.0
    values = jax.random.normal(rng, shape, jnp.float32) * width * loudness
    return jnp.minimum(jnp.maximum(values, -limit), limit).astype(kind)


def setup_inputs(seed: int = 0) -> dict:
    streams_of = jax.random.split(jax.random.key(seed), 5)
    qkv = draw_qkv(jax.random.fold_in(streams_of[4], 71), 0)
    token_rate = jnp.clip(jnp.exp(math.log(1.0) - 2.3025851 * jax.random.uniform(streams_of[1], (TOKENS, HEADS), jnp.float32) ** steps_of(streams_of[1], (TOKENS, HEADS), ((0, 16), (1, 2)), -0.2, 0.2)), 0.1, 1.0)
    head_rate = jnp.clip(jnp.exp(math.log(2.0) - 1.3862944 * jax.random.uniform(streams_of[2], (HEADS,), jnp.float32) ** steps_of(streams_of[2], (HEADS,), ((0, 2),), -0.2, 0.2)), 0.5, 2.0)
    fast_state = bell_draw(streams_of[3], (3, HEADS, FH, HD), HD ** -0.5, 0.25, ((1, 2), (2, 16)), jnp.float32)
    return {"qkv": qkv, "token_rate": token_rate, "head_rate": head_rate, "fast_state": fast_state}


ns_first = 3.4445
ns_second = -4.775
ns_third = 2.0315
rms_eps = 1e-06
norm_eps = 1e-07
precise = lax.Precision.HIGHEST

def rms_scaled(values):
    return values * lax.rsqrt(lax.optimization_barrier(jnp.mean(values * values, axis=-1, keepdims=True)) + rms_eps)

def contract_last(left_side, right_side):
    return lax.dot_general(left_side, right_side, (((1,), (1,)), ((), ())), preferred_element_type=jnp.float32)

def contract_first(left_side, right_side):
    return lax.dot_general(left_side, right_side, (((0,), (0,)), ((), ())), preferred_element_type=jnp.float32)

def head_gradient(key_norm, signal, weight_piece):
    gate_act = contract_last(key_norm, weight_piece[0])
    up_act = contract_last(key_norm, weight_piece[1])
    active = (jax.nn.silu(gate_act) * up_act).astype(jnp.bfloat16)
    back_grad = contract_last(signal, weight_piece[2])
    sigmoid_gate = jax.nn.sigmoid(gate_act)
    grad_gate = (back_grad * up_act * sigmoid_gate * (1.0 + gate_act * (1.0 - sigmoid_gate))).astype(jnp.bfloat16)
    grad_up = (back_grad * jax.nn.silu(gate_act)).astype(jnp.bfloat16)
    return jnp.stack([contract_first(grad_gate, key_norm), contract_first(grad_up, key_norm), contract_first(active, signal)])

def window_attention(queries, keys_head, values_head):
    pad_rows = jnp.zeros((WINDOW, HD), jnp.bfloat16)
    padded_keys = jnp.concatenate([pad_rows, keys_head], axis=0)
    padded_values = jnp.concatenate([pad_rows, values_head], axis=0)
    starts = jnp.arange(TOKENS // TOK_DEV, dtype=jnp.int32) * TOK_DEV

    def one_block(block_start):
        query_block = lax.dynamic_slice_in_dim(queries, block_start, TOK_DEV, 0)
        key_block = lax.dynamic_slice_in_dim(padded_keys, block_start, WINDOW + TOK_DEV, 0)
        value_block = lax.dynamic_slice_in_dim(padded_values, block_start, WINDOW + TOK_DEV, 0)
        scores = contract_last(query_block, key_block) * HD ** (-0.5)
        query_pos = block_start + jnp.arange(TOK_DEV, dtype=jnp.int32)[:, None]
        key_pos = block_start - WINDOW + jnp.arange(WINDOW + TOK_DEV, dtype=jnp.int32)[None, :]
        visible = (key_pos <= query_pos) & (key_pos > query_pos - WINDOW) & (key_pos >= 0)
        scores = jnp.where(visible, scores, -jnp.inf)
        row_max = lax.optimization_barrier(jnp.max(scores, axis=1, keepdims=True))
        exp_scores = jnp.exp(scores - row_max)
        weights = (exp_scores / lax.optimization_barrier(jnp.sum(exp_scores, axis=1, keepdims=True))).astype(jnp.bfloat16)
        return jnp.dot(weights, value_block, preferred_element_type=jnp.float32)
    return lax.map(one_block, starts).reshape(TOKENS, HD)

def newton_schulz(gradients):
    frob_norm = jnp.sqrt(lax.optimization_barrier(jnp.sum(gradients * gradients, axis=(1, 2), keepdims=True)))
    iterate = gradients / (frob_norm + norm_eps)
    for section_number in range(NS_STEPS):
        gram_matrix = jnp.einsum('mij,mkj->mik', iterate, iterate, precision=precise)
        poly_part = ns_second * gram_matrix + ns_third * jnp.einsum('mij,mjk->mik', gram_matrix, gram_matrix, precision=precise)
        iterate = ns_first * iterate + jnp.einsum('mij,mjk->mik', poly_part, iterate, precision=precise)
    return iterate

def one_head(packed):
    queries, keys_head, values_head, token_rates, step_size, head_state = packed
    query_norm = rms_scaled(queries.astype(jnp.float32)).astype(jnp.bfloat16)
    key_norm = rms_scaled(keys_head.astype(jnp.float32)).astype(jnp.bfloat16)
    signal = (-token_rates[:, None] * values_head.astype(jnp.float32)).astype(jnp.bfloat16)
    gradients = head_gradient(key_norm, signal, head_state.astype(jnp.bfloat16))
    updated = head_state - step_size * newton_schulz(gradients)
    new_low = updated.astype(jnp.bfloat16)
    gate_act = contract_last(query_norm, new_low[0])
    up_act = contract_last(query_norm, new_low[1])
    active = (jax.nn.silu(gate_act) * up_act).astype(jnp.bfloat16)
    fast_out = jnp.dot(active, new_low[2], preferred_element_type=jnp.float32)
    attention = window_attention(queries, keys_head, values_head)
    return ((attention + fast_out).astype(jnp.bfloat16), updated)

def reference(qkv, token_rate, head_rate, fast_state):
    split_heads = qkv.reshape(3, TOKENS, HEADS, HD).transpose(0, 2, 1, 3)
    outputs, states = lax.map(one_head, (split_heads[0], split_heads[1], split_heads[2], token_rate.T, head_rate, fast_state.transpose(1, 0, 2, 3)))
    combined = outputs.transpose(1, 0, 2).reshape(TOKENS, HEADS * HD)
    return (combined, states.transpose(1, 0, 2, 3))
```

```python
import jax
import jax.numpy as jnp
from jax import lax
from jax.sharding import PartitionSpec as P

WINDOW = 1024
NS_STEPS = 2


ns_first = 3.4445
ns_second = -4.775
ns_third = 2.0315
rms_eps = 1e-06
norm_eps = 1e-07


def rms_scaled(values):
    return values * lax.rsqrt(jnp.mean(values * values, axis=-1, keepdims=True) + rms_eps)


def contract_last(left_side, right_side):
    return lax.dot_general(
        left_side, right_side, (((1,), (1,)), ((), ())), preferred_element_type=jnp.float32
    )


def contract_first(left_side, right_side):
    return lax.dot_general(
        left_side, right_side, (((0,), (0,)), ((), ())), preferred_element_type=jnp.float32
    )


def row_gradient(key_norm, signal, weight_rows):
    gate_act = contract_last(key_norm, weight_rows[0])
    up_act = contract_last(key_norm, weight_rows[1])
    back_grad = contract_last(signal, weight_rows[2])
    sigmoid_gate = jax.nn.sigmoid(gate_act)
    silu_gate = gate_act * sigmoid_gate
    active = (silu_gate * up_act).astype(jnp.bfloat16)
    grad_gate = (
        back_grad * up_act * sigmoid_gate * (1.0 + gate_act * (1.0 - sigmoid_gate))
    ).astype(jnp.bfloat16)
    grad_up = (back_grad * silu_gate).astype(jnp.bfloat16)
    return jnp.stack(
        [
            contract_first(grad_gate, key_norm),
            contract_first(grad_up, key_norm),
            contract_first(active, signal),
        ]
    )


def low_dot(left_side, right_side, subscripts):
    return jnp.einsum(
        subscripts,
        left_side.astype(jnp.bfloat16),
        right_side.astype(jnp.bfloat16),
        preferred_element_type=jnp.float32,
    )


def newton_schulz(gradients):
    frob_norm = jnp.sqrt(jnp.sum(gradients * gradients, axis=(1, 2), keepdims=True))
    iterate = gradients / (frob_norm + norm_eps)
    for _ in range(NS_STEPS):
        gram = low_dot(iterate, iterate, "mij,mkj->mik")
        poly = ns_second * gram + ns_third * low_dot(gram, gram, "mij,mjk->mik")
        iterate = ns_first * iterate + low_dot(poly, iterate, "mij,mjk->mik")
    return iterate


def shards(qkv, token_rate, head_rate, fast_state):
    grouped = lax.all_to_all(qkv, "head", split_axis=2, concat_axis=1, tiled=True)
    tok_rows = grouped.shape[1]
    head_dim = grouped.shape[2]
    seq_index = lax.axis_index("seq")
    state_rows = fast_state.shape[2]
    query_norm = rms_scaled(grouped[0].astype(jnp.float32)).astype(jnp.bfloat16)
    gathered = lax.all_gather(grouped[1:3], "seq", axis=1, tiled=True)
    rates = lax.all_gather(token_rate, "seq", axis=0, tiled=True)
    key_norm = rms_scaled(gathered[0].astype(jnp.float32)).astype(jnp.bfloat16)
    signal = (-rates * gathered[1].astype(jnp.float32)).astype(jnp.bfloat16)
    old_state = fast_state[:, 0]
    old_low = old_state.astype(jnp.bfloat16)
    old_full = lax.all_gather(old_low, "seq", axis=1, tiled=True)
    own_rows = row_gradient(key_norm, signal, old_low)
    summed = lax.all_gather(own_rows.astype(jnp.bfloat16), "seq", axis=1, tiled=True)
    direction = head_rate[0] * newton_schulz(summed.astype(jnp.float32))
    new_rows = old_state - lax.dynamic_slice_in_dim(
        direction, seq_index * state_rows, state_rows, 1
    )
    weight_piece = (old_full.astype(jnp.float32) - direction).astype(jnp.bfloat16)
    gate_act = contract_last(query_norm, weight_piece[0])
    up_act = contract_last(query_norm, weight_piece[1])
    active = (jax.nn.silu(gate_act) * up_act).astype(jnp.bfloat16)
    fast_out = jnp.dot(active, weight_piece[2], preferred_element_type=jnp.float32)
    span = WINDOW + tok_rows
    padded = jnp.pad(gathered, ((0, 0), (WINDOW, 0), (0, 0)))
    context = lax.dynamic_slice_in_dim(padded, seq_index * tok_rows, span, 1)
    scores = contract_last(grouped[0], context[0]) * head_dim ** (-0.5)
    query_pos = seq_index * tok_rows + jnp.arange(tok_rows, dtype=jnp.int32)[:, None]
    key_pos = (
        seq_index * tok_rows - WINDOW + jnp.arange(WINDOW + tok_rows, dtype=jnp.int32)[None, :]
    )
    visible = (key_pos <= query_pos) & (key_pos > query_pos - WINDOW) & (key_pos >= 0)
    scores = jnp.where(visible, scores, -jnp.inf)
    row_max = jnp.max(scores, axis=1, keepdims=True)
    exp_scores = jnp.exp(scores - row_max)
    weights = (exp_scores / jnp.sum(exp_scores, axis=1, keepdims=True)).astype(jnp.bfloat16)
    attention = jnp.dot(weights, context[1], preferred_element_type=jnp.float32)
    combined = (attention + fast_out).astype(jnp.bfloat16)
    tokens_back = lax.all_to_all(combined, "head", split_axis=0, concat_axis=1, tiled=True)
    return (tokens_back, new_rows[:, None])


def solution(mesh):
    return jax.shard_map(
        shards,
        mesh=mesh,
        in_specs=(
            P(None, ("seq", "head"), None),
            P("seq", "head"),
            P("head"),
            P(None, "head", "seq", None),
        ),
        out_specs=(P(("seq", "head"), None), P(None, "head", "seq", None)),
        check_vma=False,
    )
```

```python
import functools

import jax
import jax.numpy as jnp
from jax import lax
from jax.experimental import pallas as pl
from jax.experimental.pallas import tpu as pltpu
from jax.sharding import PartitionSpec as P

WINDOW = 1024
NS_STEPS = 2
MESH = pl.DeviceIdType.MESH

ns_first = 3.4445
ns_second = -4.775
ns_third = 2.0315
rms_eps = 1e-06
norm_eps = 1e-07

BF = jnp.bfloat16
F32 = jnp.float32


def rms_scaled(values):
    return values * lax.rsqrt(jnp.mean(values * values, axis=-1, keepdims=True) + rms_eps)


def dot_nt(left, right):
    return lax.dot_general(left, right, (((1,), (1,)), ((), ())), preferred_element_type=F32)


def dot_nn(left, right):
    return lax.dot_general(left, right, (((1,), (0,)), ((), ())), preferred_element_type=F32)


def kernel(
    S, H, wire,
    qkv_ref, rate_ref, hr_ref, state_ref,
    out_ref, new_ref,
    qbuf, kbuf, vbuf, rbuf, wbuf, gbuf, scores, acc_a, acc_b, attn, comb, xbuf,
    x_send, x_recv, o_send, o_recv, loc,
    r_send, r_recv, l_send, l_recv, p_send, p_recv,
):
    C = S // 2
    half = C // 2
    tok_rows, hd = qbuf.shape
    blk = tok_rows // H
    rows = state_ref.shape[1]
    fh = S * rows
    s = lax.axis_index("seq")
    h = lax.axis_index("head")
    chip, core = s // 2, s % 2
    row_y, row_z = chip % 2, chip // 2
    pos = (1 - row_y) * row_z + row_y * (C - 1 - row_z)

    def seq_of(q, which):
        far = q // half
        return 2 * ((1 - far) * (2 * q) + far * (2 * (C - 1 - q) + 1)) + which

    right = seq_of((pos + 1) % C, core)
    left = seq_of((pos + C - 1) % C, core)
    partner = chip * 2 + 1 - core
    others = [(h + j) % H for j in range(1, H)]

    barrier = pltpu.get_barrier_semaphore()
    for target in (right, left, partner):
        pl.semaphore_signal(barrier, inc=1, device_id=(target, h), device_id_type=MESH)
    for o in others:
        pl.semaphore_signal(barrier, inc=1, device_id=(s, o), device_id_type=MESH)
    wbuf[:, 0] = state_ref[...].astype(wire)
    rbuf[0] = rate_ref[...]
    pl.semaphore_wait(barrier, 3 + H - 1)

    def mine(o):
        return pl.ds(pl.multiple_of(o * blk, blk), blk)

    def cols(o):
        return pl.ds(pl.multiple_of(o * hd, hd), hd)

    parts = [(1, lambda: kbuf.at[0]), (2, lambda: vbuf.at[0]), (0, lambda: qbuf)]
    entry, local = {}, {}
    for which, dst in parts:
        for j, o in enumerate(others):
            entry[which, j] = pltpu.make_async_remote_copy(
                src_ref=qkv_ref.at[which, :, cols(o)],
                dst_ref=dst().at[mine(h)],
                send_sem=x_send.at[which, j], recv_sem=x_recv.at[which, j],
                device_id=(s, o), device_id_type=MESH,
            )
            entry[which, j].start()
        local[which] = pltpu.make_async_copy(
            qkv_ref.at[which, :, cols(h)], dst().at[mine(h)], loc.at[which]
        )
        local[which].start()

    up, down = half, C - 1 - half
    items = {
        "w": (0, lambda i: wbuf.at[:, i], down, up),
        "k": (1, lambda i: kbuf.at[i], up, down),
        "v": (2, lambda i: vbuf.at[i], down, up),
        "r": (3, lambda i: rbuf.at[i], up, down),
        "g0": (4, lambda i: gbuf.at[0, i], up, down),
        "g1": (5, lambda i: gbuf.at[1, i], down, up),
        "g2": (6, lambda i: gbuf.at[2, i], up, down),
    }
    sends = []
    pending = {}

    def remote(src, dst, ss, rs, target):
        copy = pltpu.make_async_remote_copy(
            src_ref=src, dst_ref=dst, send_sem=ss, recv_sem=rs,
            device_id=(target, h), device_id_type=MESH,
        )
        copy.start()
        sends.append(copy)
        return copy

    def to_partner(name, d):
        n, at, _, _ = items[name]
        pending["p", name, d] = remote(
            at(d), at(C + d), p_send.at[n, d], p_recv.at[n, d], partner
        )

    def ring(name, t):
        n, at, nr, nl = items[name]
        if 0 < t <= nr:
            pending["r", name, t - 1].wait_recv()
        if t < nr:
            pending["r", name, t] = remote(
                at((C - t) % C), at(C - t - 1), r_send.at[n, t], r_recv.at[n, t], right
            )
        if 0 < t <= nl:
            pending["l", name, t - 1].wait_recv()
        if t < nl:
            pending["l", name, t] = remote(
                at(t), at(t + 1), l_send.at[n, t], l_recv.at[n, t], left
            )
        if t == 0:
            to_partner(name, 0)
        if 0 < t <= nr:
            to_partner(name, C - t)
        if 0 < t <= nl:
            to_partner(name, t)

    def from_partner(name, d):
        pending["p", name, d].wait_recv()

    q_pos = s * tok_rows + lax.broadcasted_iota(jnp.int32, (tok_rows, tok_rows), 0)
    k_iota = lax.broadcasted_iota(jnp.int32, (tok_rows, tok_rows), 1)
    w_low = state_ref[...].astype(BF)
    w_gate_up = w_low[0:2].reshape(2 * rows, hd)
    w_down = w_low[2]
    acc_a[...] = jnp.zeros_like(acc_a)
    acc_b[...] = jnp.zeros_like(acc_b)

    def process(slot, origin):
        keys = kbuf[slot]
        values = vbuf[slot]
        key_norm = rms_scaled(keys.astype(F32)).astype(BF)
        neg_rate = -rbuf[slot]
        gate_up = dot_nt(w_gate_up, key_norm)
        gate, up_act = gate_up[:rows], gate_up[rows:]
        back = dot_nt(w_down, values) * neg_rate
        sig = jax.nn.sigmoid(gate)
        silu = gate * sig
        grad_gate = back * up_act * sig * (1.0 + gate * (1.0 - sig))
        grad_up = back * silu
        both = jnp.concatenate([grad_gate, grad_up], axis=0).astype(BF)
        acc_a[...] += dot_nn(both, key_norm)
        acc_b[...] += dot_nn((silu * up_act * neg_rate).astype(BF), values)
        sc = dot_nt(qbuf[...], keys) * hd ** (-0.5)
        k_pos = origin * tok_rows + k_iota
        visible = (k_pos <= q_pos) & (k_pos > q_pos - WINDOW)
        scores[:, slot * tok_rows:(slot + 1) * tok_rows] = jnp.where(visible, sc, -jnp.inf)

    def process_own(d):
        process(d, seq_of((pos + d) % C, core))

    def process_partner(d):
        for name in ("k", "v", "r"):
            from_partner(name, d)
        process(C + d, seq_of((pos + d) % C, 1 - core))

    ring("w", 0)
    for which in (1, 2):
        local[which].wait()
        for j in range(H - 1):
            entry[which, j].wait_recv()
    for name in ("k", "v", "r"):
        ring(name, 0)
    local[0].wait()
    for j in range(H - 1):
        entry[0, j].wait_recv()
    ring_slots = [[0]]
    for t in range(1, half + 1):
        ring_slots.append(sorted({C - t, t}))
    for t in range(half + 1):
        if t > 0:
            for name in ("w", "k", "v", "r"):
                ring(name, t)
        if t > 0:
            for d in ring_slots[t - 1]:
                process_partner(d)
        for d in ring_slots[t]:
            process_own(d)
    for d in ring_slots[half]:
        process_partner(d)

    gbuf[0, 0] = acc_a[:rows].astype(wire)
    gbuf[1, 0] = acc_a[rows:].astype(wire)
    gbuf[2, 0] = acc_b[...].astype(wire)
    grads = ("g0", "g1", "g2")
    for name in grads:
        ring(name, 0)
    row_max = jnp.max(scores[...], axis=1, keepdims=True)
    scores[...] = jnp.exp(scores[...] - row_max)
    for t in range(1, half + 1):
        for name in grads:
            ring(name, t)
        if t == 1:
            total = jnp.sum(scores[...], axis=1, keepdims=True)
            weights = (scores[...] / total).astype(BF)
            attn[...] = dot_nn(weights, vbuf[...].reshape(S * tok_rows, hd))
    for d in range(C):
        from_partner("w", d)
        for name in grads:
            from_partner(name, d)
    for copy in sends:
        copy.wait_send()
    for copy in entry.values():
        copy.wait_send()

    rate = hr_ref[0]

    def update(m, carry):
        grad = gbuf[m].reshape(fh, hd).astype(F32)
        frob = jnp.sqrt(jnp.sum(grad * grad, keepdims=True))
        xbuf[...] = grad / (frob + norm_eps)
        for _ in range(NS_STEPS):
            low = xbuf[...].astype(BF)
            gram = dot_nt(low, low)
            gram_low = gram.astype(BF)
            poly = ns_second * gram + ns_third * dot_nn(gram_low, gram_low)
            xbuf[...] = ns_first * xbuf[...] + dot_nn(poly.astype(BF), low)
        new_ref[m] = state_ref[m] - rate * xbuf[0:rows]
        fresh = wbuf[m].reshape(fh, hd).astype(F32) - rate * xbuf[...]
        wbuf[m] = fresh.astype(wire).reshape(S, rows, hd)
        return carry

    lax.fori_loop(0, 3, update, 0)

    query_norm = rms_scaled(qbuf[...].astype(F32)).astype(BF)
    gate_q = dot_nt(query_norm, wbuf[0].reshape(fh, hd).astype(BF))
    up_q = dot_nt(query_norm, wbuf[1].reshape(fh, hd).astype(BF))
    active_q = (jax.nn.silu(gate_q) * up_q).astype(BF)
    fast_out = dot_nn(active_q, wbuf[2].reshape(fh, hd).astype(BF))
    comb[...] = (attn[...] + fast_out).astype(BF)
    back_copies = []
    for j, o in enumerate(others):
        copy = pltpu.make_async_remote_copy(
            src_ref=comb.at[mine(o)], dst_ref=out_ref.at[:, cols(h)],
            send_sem=o_send.at[j], recv_sem=o_recv.at[j],
            device_id=(s, o), device_id_type=MESH,
        )
        copy.start()
        back_copies.append(copy)
    own = pltpu.make_async_copy(comb.at[mine(h)], out_ref.at[:, cols(h)], loc.at[3])
    own.start()
    own.wait()
    for copy in back_copies:
        copy.wait()


def shards(S, H, qkv, token_rate, head_rate, fast_state):
    hd = qkv.shape[2] // H
    blk = qkv.shape[1]
    tok_rows = blk * H
    rows = fast_state.shape[2]
    wire = BF if rows % 16 == 0 else F32
    C = S // 2
    half = max(C // 2, 1)
    dma = pltpu.SemaphoreType.DMA
    vmem = pl.BlockSpec(memory_space=pltpu.VMEM)
    out, new_rows = pl.pallas_call(
        functools.partial(kernel, S, H, wire),
        out_shape=(
            jax.ShapeDtypeStruct((blk, H * hd), BF),
            jax.ShapeDtypeStruct((3, rows, hd), F32),
        ),
        in_specs=[vmem, vmem, pl.BlockSpec(memory_space=pltpu.SMEM), vmem],
        out_specs=(vmem, vmem),
        scratch_shapes=[
            pltpu.VMEM((tok_rows, hd), BF),
            pltpu.VMEM((S, tok_rows, hd), BF),
            pltpu.VMEM((S, tok_rows, hd), BF),
            pltpu.VMEM((S, 1, tok_rows), F32),
            pltpu.VMEM((3, S, rows, hd), wire),
            pltpu.VMEM((3, S, rows, hd), wire),
            pltpu.VMEM((tok_rows, S * tok_rows), F32),
            pltpu.VMEM((2 * rows, hd), F32),
            pltpu.VMEM((rows, hd), F32),
            pltpu.VMEM((tok_rows, hd), F32),
            pltpu.VMEM((tok_rows, hd), BF),
            pltpu.VMEM((S * rows, hd), F32),
            dma((3, max(H - 1, 1))), dma((3, max(H - 1, 1))),
            dma((max(H - 1, 1),)), dma((max(H - 1, 1),)), dma((4,)),
            dma((7, half)), dma((7, half)), dma((7, half)), dma((7, half)),
            dma((7, C)), dma((7, C)),
        ],
        compiler_params=pltpu.CompilerParams(collective_id=0, has_side_effects=True),
    )(qkv, token_rate.reshape(1, tok_rows), head_rate, fast_state[:, 0])
    return (out, new_rows[:, None])


def solution(mesh):
    return jax.shard_map(
        functools.partial(shards, mesh.shape["seq"], mesh.shape["head"]),
        mesh=mesh,
        in_specs=(
            P(None, ("seq", "head"), None),
            P("seq", "head"),
            P("head"),
            P(None, "head", "seq", None),
        ),
        out_specs=(P(("seq", "head"), None), P(None, "head", "seq", None)),
        check_vma=False,
    )
```

```python
import functools

import jax
import jax.numpy as jnp
from jax import lax
from jax.experimental import pallas as pl
from jax.experimental.pallas import tpu as pltpu
from jax.sharding import PartitionSpec as P

WINDOW = 1024
NS_STEPS = 2
MESH = pl.DeviceIdType.MESH

ns_first = 3.4445
ns_second = -4.775
ns_third = 2.0315
rms_eps = 1e-06
norm_eps = 1e-07

BF = jnp.bfloat16
F32 = jnp.float32


def rms_scaled(values):
    return values * lax.rsqrt(jnp.mean(values * values, axis=-1, keepdims=True) + rms_eps)


def dot_nt(left, right):
    return lax.dot_general(left, right, (((1,), (1,)), ((), ())), preferred_element_type=F32)


def dot_nn(left, right):
    return lax.dot_general(left, right, (((1,), (0,)), ((), ())), preferred_element_type=F32)


def kernel(
    S, H, wire,
    qkv_ref, rate_ref, hr_ref, state_ref,
    out_ref, new_ref,
    qbuf, kbuf, vbuf, rbuf, wbuf, gbuf, scores, acc_a, acc_b, attn, comb, xbuf,
    x_send, x_recv, o_send, o_recv, loc,
    r_send, r_recv, l_send, l_recv, p_send, p_recv,
):
    C = S // 2
    half = C // 2
    tok_rows, hd = qbuf.shape
    blk = tok_rows // H
    rows = state_ref.shape[1]
    fh = S * rows
    s = lax.axis_index("seq")
    h = lax.axis_index("head")
    chip, core = s // 2, s % 2
    row_y, row_z = chip % 2, chip // 2
    pos = (1 - row_y) * row_z + row_y * (C - 1 - row_z)

    def seq_of(q, which):
        far = q // half
        return 2 * ((1 - far) * (2 * q) + far * (2 * (C - 1 - q) + 1)) + which

    right = seq_of((pos + 1) % C, core)
    left = seq_of((pos + C - 1) % C, core)
    partner = chip * 2 + 1 - core
    others = [(h + j) % H for j in range(1, H)]

    barrier = pltpu.get_barrier_semaphore()
    for target in (right, left, partner):
        pl.semaphore_signal(barrier, inc=1, device_id=(target, h), device_id_type=MESH)
    for o in others:
        pl.semaphore_signal(barrier, inc=1, device_id=(s, o), device_id_type=MESH)
    wbuf[:, 0] = state_ref[...].astype(wire)
    rbuf[0] = rate_ref[...]
    pl.semaphore_wait(barrier, 3 + H - 1)

    def mine(o):
        return pl.ds(pl.multiple_of(o * blk, blk), blk)

    def cols(o):
        return pl.ds(pl.multiple_of(o * hd, hd), hd)

    parts = [(1, lambda: kbuf.at[0]), (2, lambda: vbuf.at[0]), (0, lambda: qbuf)]
    entry, local = {}, {}
    for which, dst in parts:
        for j, o in enumerate(others):
            entry[which, j] = pltpu.make_async_remote_copy(
                src_ref=qkv_ref.at[which, :, cols(o)],
                dst_ref=dst().at[mine(h)],
                send_sem=x_send.at[which, j], recv_sem=x_recv.at[which, j],
                device_id=(s, o), device_id_type=MESH,
            )
            entry[which, j].start()
        local[which] = pltpu.make_async_copy(
            qkv_ref.at[which, :, cols(h)], dst().at[mine(h)], loc.at[which]
        )
        local[which].start()

    up, down = half, C - 1 - half
    spans = [mine(h), mine(others[0])] if H == 2 else [slice(None)]
    items = {"r": (0, lambda i: rbuf.at[i], up, down), "w": (1, lambda i: wbuf.at[:, i], down, up)}
    for m in range(3):
        lanes = (down, up) if m == 1 else (up, down)
        items["g", m] = (2 + m, lambda i, m=m: gbuf.at[m, i], *lanes)
    for j, span in enumerate(spans):
        items["k", j] = (5 + 2 * j, lambda i, span=span: kbuf.at[i, span], up, down)
        items["v", j] = (6 + 2 * j, lambda i, span=span: vbuf.at[i, span], down, up)
    first = [("k", 0), ("v", 0), "r"]
    second = [("k", j) for j in range(1, len(spans))] + [("v", j) for j in range(1, len(spans))]
    grads = [("g", m) for m in range(3)]
    sends = []
    pending = {}

    def remote(src, dst, ss, rs, target):
        copy = pltpu.make_async_remote_copy(
            src_ref=src, dst_ref=dst, send_sem=ss, recv_sem=rs,
            device_id=(target, h), device_id_type=MESH,
        )
        copy.start()
        sends.append(copy)
        return copy

    def to_partner(name, d):
        n, at, _, _ = items[name]
        pending["p", name, d] = remote(
            at(d), at(C + d), p_send.at[n, d], p_recv.at[n, d], partner
        )

    def ring(name, t):
        n, at, nr, nl = items[name]
        if 0 < t <= nr:
            pending["r", name, t - 1].wait_recv()
        if t < nr:
            pending["r", name, t] = remote(
                at((C - t) % C), at(C - t - 1), r_send.at[n, t], r_recv.at[n, t], right
            )
        if 0 < t <= nl:
            pending["l", name, t - 1].wait_recv()
        if t < nl:
            pending["l", name, t] = remote(
                at(t), at(t + 1), l_send.at[n, t], l_recv.at[n, t], left
            )
        if t == 0:
            to_partner(name, 0)
        if 0 < t <= nr:
            to_partner(name, C - t)
        if 0 < t <= nl:
            to_partner(name, t)

    def from_partner(name, d):
        pending["p", name, d].wait_recv()

    q_pos = s * tok_rows + lax.broadcasted_iota(jnp.int32, (tok_rows, tok_rows), 0)
    k_iota = lax.broadcasted_iota(jnp.int32, (tok_rows, tok_rows), 1)
    w_low = state_ref[...].astype(BF)
    w_gate_up = w_low[0:2].reshape(2 * rows, hd)
    w_down = w_low[2]
    acc_a[...] = jnp.zeros_like(acc_a)
    acc_b[...] = jnp.zeros_like(acc_b)

    def process(slot, origin):
        keys = kbuf[slot]
        values = vbuf[slot]
        key_norm = rms_scaled(keys.astype(F32)).astype(BF)
        neg_rate = -rbuf[slot]
        gate_up = dot_nt(w_gate_up, key_norm)
        gate, up_act = gate_up[:rows], gate_up[rows:]
        back = dot_nt(w_down, values) * neg_rate
        sig = jax.nn.sigmoid(gate)
        silu = gate * sig
        grad_gate = back * up_act * sig * (1.0 + gate * (1.0 - sig))
        grad_up = back * silu
        both = jnp.concatenate([grad_gate, grad_up], axis=0).astype(BF)
        acc_a[...] += dot_nn(both, key_norm)
        acc_b[...] += dot_nn((silu * up_act * neg_rate).astype(BF), values)
        sc = dot_nt(qbuf[...], keys) * hd ** (-0.5)
        k_pos = origin * tok_rows + k_iota
        visible = (k_pos <= q_pos) & (k_pos > q_pos - WINDOW)
        scores[:, slot * tok_rows:(slot + 1) * tok_rows] = jnp.where(visible, sc, -jnp.inf)

    def process_own(d):
        process(d, seq_of((pos + d) % C, core))

    def process_partner(d):
        for name in first + second:
            from_partner(name, d)
        process(C + d, seq_of((pos + d) % C, 1 - core))

    for which in (1, 2):
        local[which].wait()
    if H == 2:
        for name in first:
            ring(name, 0)
    ring("w", 0)
    for which in (1, 2):
        for j in range(H - 1):
            entry[which, j].wait_recv()
    for name in second if H == 2 else first:
        ring(name, 0)
    local[0].wait()
    for j in range(H - 1):
        entry[0, j].wait_recv()
    ring_slots = [[0]]
    for t in range(1, half + 1):
        ring_slots.append(sorted({C - t, t}))
    for t in range(half + 1):
        if t > 0:
            for name in first + second:
                ring(name, t)
        if t == half - 1:
            for late in range(1, half - 2):
                ring("w", late)
        if t > 0:
            for d in ring_slots[t - 1]:
                process_partner(d)
        for d in ring_slots[t]:
            process_own(d)
        if t == half:
            ring("w", half - 2)
    for d in ring_slots[half]:
        process_partner(d)

    gbuf[0, 0] = acc_a[:rows].astype(wire)
    gbuf[1, 0] = acc_a[rows:].astype(wire)
    gbuf[2, 0] = acc_b[...].astype(wire)
    for name in grads:
        ring(name, 0)
    row_max = jnp.max(scores[...], axis=1, keepdims=True)
    scores[...] = jnp.exp(scores[...] - row_max)
    for t in range(1, half + 1):
        for name in grads:
            ring(name, t)
        if t == half - 1:
            ring("w", half - 1)
        if t == 1:
            total = jnp.sum(scores[...], axis=1, keepdims=True)
            weights = (scores[...] / total).astype(BF)
            attn[...] = dot_nn(weights, vbuf[...].reshape(S * tok_rows, hd))
    for d in range(C):
        for name in grads:
            from_partner(name, d)
    rate = hr_ref[0]

    def orthogonal(m):
        grad = gbuf[m].reshape(fh, hd).astype(F32)
        frob = jnp.sqrt(jnp.sum(grad * grad, keepdims=True))
        xbuf[m] = grad / (frob + norm_eps)
        for _ in range(NS_STEPS):
            low = xbuf[m].astype(BF)
            gram = dot_nt(low, low)
            gram_low = gram.astype(BF)
            poly = ns_second * gram + ns_third * dot_nn(gram_low, gram_low)
            xbuf[m] = ns_first * xbuf[m] + dot_nn(poly.astype(BF), low)
        new_ref[m] = state_ref[m] - rate * xbuf[m, 0:rows]

    def fresh(m):
        old = wbuf[m].reshape(fh, hd).astype(F32)
        return (old - rate * xbuf[m]).astype(BF)

    orthogonal(0)
    ring("w", half)
    orthogonal(1)
    orthogonal(2)
    for d in range(C):
        from_partner("w", d)

    query_norm = rms_scaled(qbuf[...].astype(F32)).astype(BF)
    gate_q = dot_nt(query_norm, fresh(0))
    up_q = dot_nt(query_norm, fresh(1))
    active_q = (jax.nn.silu(gate_q) * up_q).astype(BF)
    fast_out = dot_nn(active_q, fresh(2))
    comb[...] = (attn[...] + fast_out).astype(BF)
    back_copies = []
    for j, o in enumerate(others):
        copy = pltpu.make_async_remote_copy(
            src_ref=comb.at[mine(o)], dst_ref=out_ref.at[:, cols(h)],
            send_sem=o_send.at[j], recv_sem=o_recv.at[j],
            device_id=(s, o), device_id_type=MESH,
        )
        copy.start()
        back_copies.append(copy)
    own = pltpu.make_async_copy(comb.at[mine(h)], out_ref.at[:, cols(h)], loc.at[3])
    own.start()
    own.wait()
    for copy in back_copies:
        copy.wait()
    for copy in sends:
        copy.wait_send()
    for copy in entry.values():
        copy.wait_send()


def shards(S, H, qkv, token_rate, head_rate, fast_state):
    hd = qkv.shape[2] // H
    blk = qkv.shape[1]
    tok_rows = blk * H
    rows = fast_state.shape[2]
    wire = BF if rows % 16 == 0 else F32
    C = S // 2
    half = max(C // 2, 1)
    dma = pltpu.SemaphoreType.DMA
    vmem = pl.BlockSpec(memory_space=pltpu.VMEM)
    out, new_rows = pl.pallas_call(
        functools.partial(kernel, S, H, wire),
        out_shape=(
            jax.ShapeDtypeStruct((blk, H * hd), BF),
            jax.ShapeDtypeStruct((3, rows, hd), F32),
        ),
        in_specs=[vmem, vmem, pl.BlockSpec(memory_space=pltpu.SMEM), vmem],
        out_specs=(vmem, vmem),
        scratch_shapes=[
            pltpu.VMEM((tok_rows, hd), BF),
            pltpu.VMEM((S, tok_rows, hd), BF),
            pltpu.VMEM((S, tok_rows, hd), BF),
            pltpu.VMEM((S, 1, tok_rows), F32),
            pltpu.VMEM((3, S, rows, hd), wire),
            pltpu.VMEM((3, S, rows, hd), wire),
            pltpu.VMEM((tok_rows, S * tok_rows), F32),
            pltpu.VMEM((2 * rows, hd), F32),
            pltpu.VMEM((rows, hd), F32),
            pltpu.VMEM((tok_rows, hd), F32),
            pltpu.VMEM((tok_rows, hd), BF),
            pltpu.VMEM((3, S * rows, hd), F32),
            dma((3, max(H - 1, 1))), dma((3, max(H - 1, 1))),
            dma((max(H - 1, 1),)), dma((max(H - 1, 1),)), dma((4,)),
            dma((9, half)), dma((9, half)), dma((9, half)), dma((9, half)),
            dma((9, C)), dma((9, C)),
        ],
        compiler_params=pltpu.CompilerParams(collective_id=0, has_side_effects=True),
    )(qkv, token_rate.reshape(1, tok_rows), head_rate, fast_state[:, 0])
    return (out, new_rows[:, None])


def solution(mesh):
    return jax.shard_map(
        functools.partial(shards, mesh.shape["seq"], mesh.shape["head"]),
        mesh=mesh,
        in_specs=(
            P(None, ("seq", "head"), None),
            P("seq", "head"),
            P("head"),
            P(None, "head", "seq", None),
        ),
        out_specs=(P(("seq", "head"), None), P(None, "head", "seq", None)),
        check_vma=False,
    )
```

```python
import functools

import jax
import jax.numpy as jnp
from jax import lax
from jax.experimental import pallas as pl
from jax.experimental.pallas import tpu as pltpu
from jax.sharding import PartitionSpec as P

WINDOW = 1024
NS_STEPS = 2
MESH = pl.DeviceIdType.MESH

ns_first = 3.4445
ns_second = -4.775
ns_third = 2.0315
rms_eps = 1e-06
norm_eps = 1e-07

BF = jnp.bfloat16
F32 = jnp.float32


def rms_scaled(values):
    return values * lax.rsqrt(jnp.mean(values * values, axis=-1, keepdims=True) + rms_eps)


def dot_nt(left, right):
    return lax.dot_general(left, right, (((1,), (1,)), ((), ())), preferred_element_type=F32)


def dot_nn(left, right):
    return lax.dot_general(left, right, (((1,), (0,)), ((), ())), preferred_element_type=F32)


def kernel(
    S, H, wire,
    qkv_ref, rate_ref, hr_ref, state_ref,
    out_ref, new_ref,
    qbuf, kbuf, vbuf, rbuf, wbuf, gbuf, scores, acc_a, acc_b, attn, comb, xbuf,
    x_send, x_recv, o_send, o_recv, loc,
    r_send, r_recv, l_send, l_recv, p_send, p_recv,
):
    C = S // 2
    half = C // 2
    tok_rows, hd = qbuf.shape
    blk = tok_rows // H
    rows = state_ref.shape[1]
    fh = S * rows
    s = lax.axis_index("seq")
    h = lax.axis_index("head")
    chip, core = s // 2, s % 2
    row_y, row_z = chip % 2, chip // 2
    pos = (1 - row_y) * row_z + row_y * (C - 1 - row_z)

    def seq_of(q, which):
        far = q // half
        return 2 * ((1 - far) * (2 * q) + far * (2 * (C - 1 - q) + 1)) + which

    right = seq_of((pos + 1) % C, core)
    left = seq_of((pos + C - 1) % C, core)
    partner = chip * 2 + 1 - core
    others = [(h + j) % H for j in range(1, H)]

    barrier = pltpu.get_barrier_semaphore()
    for target in (right, left, partner):
        pl.semaphore_signal(barrier, inc=1, device_id=(target, h), device_id_type=MESH)
    for o in others:
        pl.semaphore_signal(barrier, inc=1, device_id=(s, o), device_id_type=MESH)
    wbuf[:, 0] = state_ref[...].astype(wire)
    rbuf[0] = rate_ref[...]
    pl.semaphore_wait(barrier, 3 + H - 1)

    def mine(o):
        return pl.ds(pl.multiple_of(o * blk, blk), blk)

    def cols(o):
        return pl.ds(pl.multiple_of(o * hd, hd), hd)

    parts = [(1, lambda: kbuf.at[0]), (2, lambda: vbuf.at[0]), (0, lambda: qbuf)]
    entry, local = {}, {}
    for which, dst in parts:
        for j, o in enumerate(others):
            entry[which, j] = pltpu.make_async_remote_copy(
                src_ref=qkv_ref.at[which, :, cols(o)],
                dst_ref=dst().at[mine(h)],
                send_sem=x_send.at[which, j], recv_sem=x_recv.at[which, j],
                device_id=(s, o), device_id_type=MESH,
            )
            entry[which, j].start()
        local[which] = pltpu.make_async_copy(
            qkv_ref.at[which, :, cols(h)], dst().at[mine(h)], loc.at[which]
        )
        local[which].start()

    up, down = half, C - 1 - half
    spans = [mine(h), mine(others[0])] if H == 2 else [slice(None)]
    items = {"r": (0, lambda i: rbuf.at[i], up, down), "w": (1, lambda i: wbuf.at[:, i], down, up)}
    for m in range(3):
        lanes = (down, up) if m == 1 else (up, down)
        items["g", m] = (2 + m, lambda i, m=m: gbuf.at[m, i], *lanes)
    for j, span in enumerate(spans):
        items["k", j] = (5 + 2 * j, lambda i, span=span: kbuf.at[i, span], up, down)
        items["v", j] = (6 + 2 * j, lambda i, span=span: vbuf.at[i, span], down, up)
    first = [("k", 0), ("v", 0), "r"]
    second = [("k", j) for j in range(1, len(spans))] + [("v", j) for j in range(1, len(spans))]
    grads = [("g", m) for m in range(3)]
    sends = []
    pending = {}

    def remote(src, dst, ss, rs, target):
        copy = pltpu.make_async_remote_copy(
            src_ref=src, dst_ref=dst, send_sem=ss, recv_sem=rs,
            device_id=(target, h), device_id_type=MESH,
        )
        copy.start()
        sends.append(copy)
        return copy

    def to_partner(name, d):
        n, at, _, _ = items[name]
        pending["p", name, d] = remote(
            at(d), at(C + d), p_send.at[n, d], p_recv.at[n, d], partner
        )

    def ring(name, t):
        n, at, nr, nl = items[name]
        if 0 < t <= nr:
            pending["r", name, t - 1].wait_recv()
        if t < nr:
            pending["r", name, t] = remote(
                at((C - t) % C), at(C - t - 1), r_send.at[n, t], r_recv.at[n, t], right
            )
        if 0 < t <= nl:
            pending["l", name, t - 1].wait_recv()
        if t < nl:
            pending["l", name, t] = remote(
                at(t), at(t + 1), l_send.at[n, t], l_recv.at[n, t], left
            )
        if t == 0:
            to_partner(name, 0)
        if 0 < t <= nr:
            to_partner(name, C - t)
        if 0 < t <= nl:
            to_partner(name, t)

    def from_partner(name, d):
        pending["p", name, d].wait_recv()

    q_pos = s * tok_rows + lax.broadcasted_iota(jnp.int32, (tok_rows, tok_rows), 0)
    k_iota = lax.broadcasted_iota(jnp.int32, (tok_rows, tok_rows), 1)
    w_low = state_ref[...].astype(BF)
    w_gate_up = w_low[0:2].reshape(2 * rows, hd)
    w_down = w_low[2]
    acc_a[...] = jnp.zeros_like(acc_a)
    acc_b[...] = jnp.zeros_like(acc_b)

    def process(slot, origin):
        keys = kbuf[slot]
        values = vbuf[slot]
        key_norm = rms_scaled(keys.astype(F32)).astype(BF)
        neg_rate = -rbuf[slot]
        gate_up = dot_nt(w_gate_up, key_norm)
        gate, up_act = gate_up[:rows], gate_up[rows:]
        back = dot_nt(w_down, values) * neg_rate
        sig = jax.nn.sigmoid(gate)
        silu = gate * sig
        grad_gate = back * up_act * sig * (1.0 + gate * (1.0 - sig))
        grad_up = back * silu
        both = jnp.concatenate([grad_gate, grad_up], axis=0).astype(BF)
        acc_a[...] += dot_nn(both, key_norm)
        acc_b[...] += dot_nn((silu * up_act * neg_rate).astype(BF), values)
        sc = dot_nt(qbuf[...], keys) * hd ** (-0.5)
        k_pos = origin * tok_rows + k_iota
        visible = (k_pos <= q_pos) & (k_pos > q_pos - WINDOW)
        scores[:, slot * tok_rows:(slot + 1) * tok_rows] = jnp.where(visible, sc, -jnp.inf)

    def process_own(d):
        process(d, seq_of((pos + d) % C, core))

    def process_partner(d):
        for name in first + second:
            from_partner(name, d)
        process(C + d, seq_of((pos + d) % C, 1 - core))

    for which in (1, 2):
        local[which].wait()
    if H == 2:
        for name in first:
            ring(name, 0)
    ring("w", 0)
    for which in (1, 2):
        for j in range(H - 1):
            entry[which, j].wait_recv()
    for name in second if H == 2 else first:
        ring(name, 0)
    local[0].wait()
    for j in range(H - 1):
        entry[0, j].wait_recv()
    ring_slots = [[0]]
    for t in range(1, half + 1):
        ring_slots.append(sorted({C - t, t}))
    for t in range(half + 1):
        if t == half:
            for d in ring_slots[t - 1]:
                process_partner(d)
        if t > 0:
            for name in first + second:
                ring(name, t)
        if t == half - 1:
            for late in range(1, half - 2):
                ring("w", late)
        if 0 < t < half:
            for d in ring_slots[t - 1]:
                process_partner(d)
        for d in ring_slots[t]:
            process_own(d)
    for d in ring_slots[half]:
        process_partner(d)

    gbuf[0, 0] = acc_a[:rows].astype(wire)
    gbuf[1, 0] = acc_a[rows:].astype(wire)
    gbuf[2, 0] = acc_b[...].astype(wire)
    for name in grads:
        ring(name, 0)
    row_max = jnp.max(scores[...], axis=1, keepdims=True)
    scores[...] = jnp.exp(scores[...] - row_max)
    for t in range(1, half + 1):
        for name in grads:
            ring(name, t)
        if t == half - 2:
            ring("w", half - 2)
        if t == half:
            ring("w", half - 1)
        if t == 1:
            total = jnp.sum(scores[...], axis=1, keepdims=True)
            weights = (scores[...] / total).astype(BF)
            attn[...] = dot_nn(weights, vbuf[...].reshape(S * tok_rows, hd))
    for d in range(C):
        for name in grads:
            from_partner(name, d)
    rate = hr_ref[0]

    def orthogonal(m):
        grad = gbuf[m].reshape(fh, hd).astype(F32)
        frob = jnp.sqrt(jnp.sum(grad * grad, keepdims=True))
        xbuf[m] = grad / (frob + norm_eps)
        for _ in range(NS_STEPS):
            low = xbuf[m].astype(BF)
            gram = dot_nt(low, low)
            gram_low = gram.astype(BF)
            poly = ns_second * gram + ns_third * dot_nn(gram_low, gram_low)
            xbuf[m] = ns_first * xbuf[m] + dot_nn(poly.astype(BF), low)
        new_ref[m] = state_ref[m] - rate * xbuf[m, 0:rows]

    def fresh(m):
        old = wbuf[m].reshape(fh, hd).astype(F32)
        return (old - rate * xbuf[m]).astype(BF)

    orthogonal(0)
    orthogonal(1)
    ring("w", half)
    orthogonal(2)
    for d in range(C):
        from_partner("w", d)

    query_norm = rms_scaled(qbuf[...].astype(F32)).astype(BF)
    gate_q = dot_nt(query_norm, fresh(0))
    up_q = dot_nt(query_norm, fresh(1))
    active_q = (jax.nn.silu(gate_q) * up_q).astype(BF)
    fast_out = dot_nn(active_q, fresh(2))
    comb[...] = (attn[...] + fast_out).astype(BF)
    back_copies = []
    for j, o in enumerate(others):
        copy = pltpu.make_async_remote_copy(
            src_ref=comb.at[mine(o)], dst_ref=out_ref.at[:, cols(h)],
            send_sem=o_send.at[j], recv_sem=o_recv.at[j],
            device_id=(s, o), device_id_type=MESH,
        )
        copy.start()
        back_copies.append(copy)
    own = pltpu.make_async_copy(comb.at[mine(h)], out_ref.at[:, cols(h)], loc.at[3])
    own.start()
    own.wait()
    for copy in back_copies:
        copy.wait()
    for copy in sends:
        copy.wait_send()
    for copy in entry.values():
        copy.wait_send()


def shards(S, H, qkv, token_rate, head_rate, fast_state):
    hd = qkv.shape[2] // H
    blk = qkv.shape[1]
    tok_rows = blk * H
    rows = fast_state.shape[2]
    wire = BF if rows % 16 == 0 else F32
    C = S // 2
    half = max(C // 2, 1)
    dma = pltpu.SemaphoreType.DMA
    vmem = pl.BlockSpec(memory_space=pltpu.VMEM)
    out, new_rows = pl.pallas_call(
        functools.partial(kernel, S, H, wire),
        out_shape=(
            jax.ShapeDtypeStruct((blk, H * hd), BF),
            jax.ShapeDtypeStruct((3, rows, hd), F32),
        ),
        in_specs=[vmem, vmem, pl.BlockSpec(memory_space=pltpu.SMEM), vmem],
        out_specs=(vmem, vmem),
        scratch_shapes=[
            pltpu.VMEM((tok_rows, hd), BF),
            pltpu.VMEM((S, tok_rows, hd), BF),
            pltpu.VMEM((S, tok_rows, hd), BF),
            pltpu.VMEM((S, 1, tok_rows), F32),
            pltpu.VMEM((3, S, rows, hd), wire),
            pltpu.VMEM((3, S, rows, hd), wire),
            pltpu.VMEM((tok_rows, S * tok_rows), F32),
            pltpu.VMEM((2 * rows, hd), F32),
            pltpu.VMEM((rows, hd), F32),
            pltpu.VMEM((tok_rows, hd), F32),
            pltpu.VMEM((tok_rows, hd), BF),
            pltpu.VMEM((3, S * rows, hd), F32),
            dma((3, max(H - 1, 1))), dma((3, max(H - 1, 1))),
            dma((max(H - 1, 1),)), dma((max(H - 1, 1),)), dma((4,)),
            dma((9, half)), dma((9, half)), dma((9, half)), dma((9, half)),
            dma((9, C)), dma((9, C)),
        ],
        compiler_params=pltpu.CompilerParams(collective_id=0, has_side_effects=True),
    )(qkv, token_rate.reshape(1, tok_rows), head_rate, fast_state[:, 0])
    return (out, new_rows[:, None])


def solution(mesh):
    return jax.shard_map(
        functools.partial(shards, mesh.shape["seq"], mesh.shape["head"]),
        mesh=mesh,
        in_specs=(
            P(None, ("seq", "head"), None),
            P("seq", "head"),
            P("head"),
            P(None, "head", "seq", None),
        ),
        out_specs=(P(("seq", "head"), None), P(None, "head", "seq", None)),
        check_vma=False,
    )
```

```python
import functools

import jax
import jax.numpy as jnp
from jax import lax
from jax.experimental import pallas as pl
from jax.experimental.pallas import tpu as pltpu
from jax.sharding import PartitionSpec as P

WINDOW = 1024
NS_STEPS = 2
MESH = pl.DeviceIdType.MESH

ns_first = 3.4445
ns_second = -4.775
ns_third = 2.0315
rms_eps = 1e-06
norm_eps = 1e-07

BF = jnp.bfloat16
F32 = jnp.float32


def rms_scaled(values):
    return values * lax.rsqrt(jnp.mean(values * values, axis=-1, keepdims=True) + rms_eps)


def dot_nt(left, right):
    return lax.dot_general(left, right, (((1,), (1,)), ((), ())), preferred_element_type=F32)


def dot_nn(left, right):
    return lax.dot_general(left, right, (((1,), (0,)), ((), ())), preferred_element_type=F32)


def kernel(
    S, H, wire,
    qkv_ref, rate_ref, hr_ref, state_ref,
    out_ref, new_ref,
    qbuf, kbuf, vbuf, rbuf, wbuf, gbuf, scores, acc_a, acc_b, attn, comb, xbuf,
    x_send, x_recv, o_send, o_recv, loc,
    r_send, r_recv, l_send, l_recv, p_send, p_recv,
):
    C = S // 2
    half = C // 2
    tok_rows, hd = qbuf.shape
    blk = tok_rows // H
    rows = state_ref.shape[1]
    fh = S * rows
    s = lax.axis_index("seq")
    h = lax.axis_index("head")
    chip, core = s // 2, s % 2
    row_y, row_z = chip % 2, chip // 2
    pos = (1 - row_y) * row_z + row_y * (C - 1 - row_z)

    def seq_of(q, which):
        far = q // half
        return 2 * ((1 - far) * (2 * q) + far * (2 * (C - 1 - q) + 1)) + which

    right = seq_of((pos + 1) % C, core)
    left = seq_of((pos + C - 1) % C, core)
    partner = chip * 2 + 1 - core
    others = [(h + j) % H for j in range(1, H)]

    barrier = pltpu.get_barrier_semaphore()
    for target in (right, left, partner):
        pl.semaphore_signal(barrier, inc=1, device_id=(target, h), device_id_type=MESH)
    for o in others:
        pl.semaphore_signal(barrier, inc=1, device_id=(s, o), device_id_type=MESH)
    wbuf[:, 0] = state_ref[...].astype(wire)
    rbuf[0] = rate_ref[...]
    pl.semaphore_wait(barrier, 3 + H - 1)

    def mine(o):
        return pl.ds(pl.multiple_of(o * blk, blk), blk)

    def cols(o):
        return pl.ds(pl.multiple_of(o * hd, hd), hd)

    parts = [(1, lambda: kbuf.at[0]), (2, lambda: vbuf.at[0]), (0, lambda: qbuf)]
    entry, local = {}, {}
    for which, dst in parts:
        for j, o in enumerate(others):
            entry[which, j] = pltpu.make_async_remote_copy(
                src_ref=qkv_ref.at[which, :, cols(o)],
                dst_ref=dst().at[mine(h)],
                send_sem=x_send.at[which, j], recv_sem=x_recv.at[which, j],
                device_id=(s, o), device_id_type=MESH,
            )
            entry[which, j].start()
        local[which] = pltpu.make_async_copy(
            qkv_ref.at[which, :, cols(h)], dst().at[mine(h)], loc.at[which]
        )
        local[which].start()

    up, down = half, C - 1 - half
    spans = [mine(h), mine(others[0])] if H == 2 else [slice(None)]
    items = {"r": (0, lambda i: rbuf.at[i], up, down), "w": (1, lambda i: wbuf.at[:, i], down, up)}
    for m in range(3):
        lanes = (down, up) if m == 1 else (up, down)
        items["g", m] = (2 + m, lambda i, m=m: gbuf.at[m, i], *lanes)
    for j, span in enumerate(spans):
        items["k", j] = (5 + 2 * j, lambda i, span=span: kbuf.at[i, span], up, down)
        items["v", j] = (6 + 2 * j, lambda i, span=span: vbuf.at[i, span], down, up)
    first = [("k", 0), ("v", 0), "r"]
    second = [("k", j) for j in range(1, len(spans))] + [("v", j) for j in range(1, len(spans))]
    grads = [("g", m) for m in range(3)]
    sends = []
    pending = {}

    def remote(src, dst, ss, rs, target):
        copy = pltpu.make_async_remote_copy(
            src_ref=src, dst_ref=dst, send_sem=ss, recv_sem=rs,
            device_id=(target, h), device_id_type=MESH,
        )
        copy.start()
        sends.append(copy)
        return copy

    def to_partner(name, d):
        n, at, _, _ = items[name]
        pending["p", name, d] = remote(
            at(d), at(C + d), p_send.at[n, d], p_recv.at[n, d], partner
        )

    def ring(name, t):
        n, at, nr, nl = items[name]
        if 0 < t <= nr:
            pending["r", name, t - 1].wait_recv()
        if t < nr:
            pending["r", name, t] = remote(
                at((C - t) % C), at(C - t - 1), r_send.at[n, t], r_recv.at[n, t], right
            )
        if 0 < t <= nl:
            pending["l", name, t - 1].wait_recv()
        if t < nl:
            pending["l", name, t] = remote(
                at(t), at(t + 1), l_send.at[n, t], l_recv.at[n, t], left
            )
        if t == 0:
            to_partner(name, 0)
        if 0 < t <= nr:
            to_partner(name, C - t)
        if 0 < t <= nl:
            to_partner(name, t)

    def from_partner(name, d):
        pending["p", name, d].wait_recv()

    q_pos = s * tok_rows + lax.broadcasted_iota(jnp.int32, (tok_rows, tok_rows), 0)
    k_iota = lax.broadcasted_iota(jnp.int32, (tok_rows, tok_rows), 1)
    w_low = state_ref[...].astype(BF)
    w_gate_up = w_low[0:2].reshape(2 * rows, hd)
    w_down = w_low[2]
    acc_a[...] = jnp.zeros_like(acc_a)
    acc_b[...] = jnp.zeros_like(acc_b)

    def process(slot, origin):
        keys = kbuf[slot]
        values = vbuf[slot]
        key_norm = rms_scaled(keys.astype(F32)).astype(BF)
        neg_rate = -rbuf[slot]
        gate_up = dot_nt(w_gate_up, key_norm)
        gate, up_act = gate_up[:rows], gate_up[rows:]
        back = dot_nt(w_down, values) * neg_rate
        sig = jax.nn.sigmoid(gate)
        silu = gate * sig
        grad_gate = back * up_act * sig * (1.0 + gate * (1.0 - sig))
        grad_up = back * silu
        both = jnp.concatenate([grad_gate, grad_up], axis=0).astype(BF)
        acc_a[...] += dot_nn(both, key_norm)
        acc_b[...] += dot_nn((silu * up_act * neg_rate).astype(BF), values)
        sc = dot_nt(qbuf[...], keys) * hd ** (-0.5)
        k_pos = origin * tok_rows + k_iota
        visible = (k_pos <= q_pos) & (k_pos > q_pos - WINDOW)
        scores[:, slot * tok_rows:(slot + 1) * tok_rows] = jnp.where(visible, sc, -jnp.inf)

    def process_own(d):
        process(d, seq_of((pos + d) % C, core))

    def process_partner(d):
        for name in first + second:
            from_partner(name, d)
        process(C + d, seq_of((pos + d) % C, 1 - core))

    for which in (1, 2):
        local[which].wait()
    if H == 2:
        for name in first:
            ring(name, 0)
    ring("w", 0)
    for which in (1, 2):
        for j in range(H - 1):
            entry[which, j].wait_recv()
    for name in second if H == 2 else first:
        ring(name, 0)
    local[0].wait()
    for j in range(H - 1):
        entry[0, j].wait_recv()
    ring_slots = [[0]]
    for t in range(1, half + 1):
        ring_slots.append(sorted({C - t, t}))
    for t in range(half + 1):
        if t == half:
            for d in ring_slots[t - 1]:
                process_partner(d)
        if t > 0:
            for name in first + second:
                ring(name, t)
        if t == half - 1:
            for late in range(1, half - 2):
                ring("w", late)
        if 0 < t < half:
            for d in ring_slots[t - 1]:
                process_partner(d)
        for d in ring_slots[t]:
            process_own(d)
    for d in ring_slots[half]:
        process_partner(d)

    gbuf[0, 0] = acc_a[:rows].astype(wire)
    gbuf[1, 0] = acc_a[rows:].astype(wire)
    gbuf[2, 0] = acc_b[...].astype(wire)
    for name in grads:
        ring(name, 0)
    row_max = jnp.max(scores[...], axis=1, keepdims=True)
    scores[...] = jnp.exp(scores[...] - row_max)
    for t in range(1, half + 1):
        for name in grads:
            ring(name, t)
        if t == half - 2:
            ring("w", half - 2)
        if t == half:
            ring("w", half - 1)
        if t == 1:
            total = jnp.sum(scores[...], axis=1, keepdims=True)
            weights = (scores[...] / total).astype(BF)
            attn[...] = dot_nn(weights, vbuf[...].reshape(S * tok_rows, hd))
    rate = hr_ref[0]

    def orthogonal(m):
        for d in range(C):
            from_partner(grads[m], d)
        grad = gbuf[m].reshape(fh, hd).astype(F32)
        frob = jnp.sqrt(jnp.sum(grad * grad, keepdims=True))
        xbuf[m] = grad / (frob + norm_eps)
        for _ in range(NS_STEPS):
            low = xbuf[m].astype(BF)
            gram = dot_nt(low, low)
            gram_low = gram.astype(BF)
            poly = ns_second * gram + ns_third * dot_nn(gram_low, gram_low)
            xbuf[m] = ns_first * xbuf[m] + dot_nn(poly.astype(BF), low)
        new_ref[m] = state_ref[m] - rate * xbuf[m, 0:rows]

    def fresh(m):
        old = wbuf[m].reshape(fh, hd).astype(F32)
        return (old - rate * xbuf[m]).astype(BF)

    orthogonal(0)
    orthogonal(1)
    ring("w", half)
    orthogonal(2)
    for d in range(C):
        from_partner("w", d)

    query_norm = rms_scaled(qbuf[...].astype(F32)).astype(BF)
    gate_q = dot_nt(query_norm, fresh(0))
    up_q = dot_nt(query_norm, fresh(1))
    active_q = (jax.nn.silu(gate_q) * up_q).astype(BF)
    fast_out = dot_nn(active_q, fresh(2))
    comb[...] = (attn[...] + fast_out).astype(BF)
    back_copies = []
    for j, o in enumerate(others):
        copy = pltpu.make_async_remote_copy(
            src_ref=comb.at[mine(o)], dst_ref=out_ref.at[:, cols(h)],
            send_sem=o_send.at[j], recv_sem=o_recv.at[j],
            device_id=(s, o), device_id_type=MESH,
        )
        copy.start()
        back_copies.append(copy)
    own = pltpu.make_async_copy(comb.at[mine(h)], out_ref.at[:, cols(h)], loc.at[3])
    own.start()
    own.wait()
    for copy in back_copies:
        copy.wait()
    for copy in sends:
        copy.wait_send()
    for copy in entry.values():
        copy.wait_send()


def shards(S, H, qkv, token_rate, head_rate, fast_state):
    hd = qkv.shape[2] // H
    blk = qkv.shape[1]
    tok_rows = blk * H
    rows = fast_state.shape[2]
    wire = BF if rows % 16 == 0 else F32
    C = S // 2
    half = max(C // 2, 1)
    dma = pltpu.SemaphoreType.DMA
    vmem = pl.BlockSpec(memory_space=pltpu.VMEM)
    out, new_rows = pl.pallas_call(
        functools.partial(kernel, S, H, wire),
        out_shape=(
            jax.ShapeDtypeStruct((blk, H * hd), BF),
            jax.ShapeDtypeStruct((3, rows, hd), F32),
        ),
        in_specs=[vmem, vmem, pl.BlockSpec(memory_space=pltpu.SMEM), vmem],
        out_specs=(vmem, vmem),
        scratch_shapes=[
            pltpu.VMEM((tok_rows, hd), BF),
            pltpu.VMEM((S, tok_rows, hd), BF),
            pltpu.VMEM((S, tok_rows, hd), BF),
            pltpu.VMEM((S, 1, tok_rows), F32),
            pltpu.VMEM((3, S, rows, hd), wire),
            pltpu.VMEM((3, S, rows, hd), wire),
            pltpu.VMEM((tok_rows, S * tok_rows), F32),
            pltpu.VMEM((2 * rows, hd), F32),
            pltpu.VMEM((rows, hd), F32),
            pltpu.VMEM((tok_rows, hd), F32),
            pltpu.VMEM((tok_rows, hd), BF),
            pltpu.VMEM((3, S * rows, hd), F32),
            dma((3, max(H - 1, 1))), dma((3, max(H - 1, 1))),
            dma((max(H - 1, 1),)), dma((max(H - 1, 1),)), dma((4,)),
            dma((9, half)), dma((9, half)), dma((9, half)), dma((9, half)),
            dma((9, C)), dma((9, C)),
        ],
        compiler_params=pltpu.CompilerParams(collective_id=0, has_side_effects=True),
    )(qkv, token_rate.reshape(1, tok_rows), head_rate, fast_state[:, 0])
    return (out, new_rows[:, None])


def solution(mesh):
    return jax.shard_map(
        functools.partial(shards, mesh.shape["seq"], mesh.shape["head"]),
        mesh=mesh,
        in_specs=(
            P(None, ("seq", "head"), None),
            P("seq", "head"),
            P("head"),
            P(None, "head", "seq", None),
        ),
        out_specs=(P(("seq", "head"), None), P(None, "head", "seq", None)),
        check_vma=False,
    )
```
